32 devices in a mesh: row: 4 (over y, x), col: 8 (over z, core).
Axes of the slice: x: 2, y: 2, z: 4, core: 2. Of those that a mesh axis runs over, the one named last changes fastest.
Arguments:
- new_row: float32 [128, 96, 128], P('row', 'col'), may hold values from -4 to 4
- history: float32 [96, 96, 128, 128], P('row', 'col'), may hold values from -0.0546875 to 0.0546875
- hamiltonian: float32 [128, 128], replicated, may hold values from -0.5 to 0.5
Outputs:
- rows_out: float32 [3, 128, 96, 128], P(None, 'row', 'col')
The draws below stay inside these ranges and needn't reach their ends.
All inputs are finite; a program needn't handle non-finite values.
Results may differ from the reference program's by a relative error of at most 0.00026.
Values sent between devices are 32-bit elements; how exact they have to be, the bound alone decides.
No kernel may reach another device: no remote copies, remote signals or barrier semaphores. Data moves between devices by JAX's collectives and lax.ppermute only.
A program may use at most 128 MiB of HBM per device.

```python
import jax
import jax.numpy as jnp
from jax import lax

NO = 128
STEPS = 3
NT = 96


def block_scale(own_key, extent, split, low, top_value):
    loudness, own = 1.0, jax.random.fold_in(own_key, 6)
    for position, shards_of in split:
        heights = jnp.exp(jax.random.uniform(jax.random.fold_in(own, position), (shards_of,), jnp.float32, low / len(split), top_value / len(split)))
        loudness = loudness * jnp.repeat(heights, extent[position] // shards_of).reshape([-1 if axis == position else 1 for axis in range(len(extent))])
    return loudness


def noise(stream_key, dims, width, bound, cuts=(), held_as=jnp.bfloat16):
    drawn = width * jax.random.normal(stream_key, dims, jnp.float32)
    if cuts:
        drawn = drawn * block_scale(stream_key, dims, cuts, -0.22, 0.18)
    return jnp.clip(drawn, -bound, bound).astype(held_as)


def setup_inputs(seed: int = 0) -> dict:
    streams_of = jax.random.split(jax.random.key(seed), 4)
    new_row = noise(streams_of[0], (NO, NT, NO), 0.7, 4.0, ((0, 4), (1, 8)), jnp.float32)
    history = noise(streams_of[1], (NT, NT, NO, NO), (NT * NO) ** -0.5, 0.0546875, ((0, 4), (1, 8)), jnp.float32)
    hamiltonian = noise(streams_of[2], (NO, NO), NO ** -0.5, 0.5, (), jnp.float32)
    return {"new_row": new_row, "history": history, "hamiltonian": hamiltonian}


time_step = 0.2


def reference(new_row, history, hamiltonian):
    current = new_row
    results = []
    for step_index in range(STEPS):
        sigma = current * current * current
        sigma_time = jnp.moveaxis(sigma, 1, 0)

        def accumulate(total, pair):
            sigma_tile, tiles = pair
            term = jnp.einsum("il,tlj->itj", sigma_tile, tiles, precision=lax.Precision.HIGHEST, preferred_element_type=jnp.float32)
            return total + term, None

        start_total = jnp.zeros(current.shape, jnp.float32)
        collision, unused = lax.scan(accumulate, start_total, (sigma_time, history))
        kinetic = jnp.einsum("itl,lj->itj", current, hamiltonian, precision=lax.Precision.HIGHEST, preferred_element_type=jnp.float32)
        current = current - time_step * (kinetic + collision)
        results.append(current)
    return jnp.stack(results)
```

```python
import functools

import jax
import jax.numpy as jnp
from jax import lax
from jax.experimental import pallas as pl
from jax.experimental.pallas import tpu as pltpu
from jax.sharding import PartitionSpec as P

STEPS = 3
CORES = 2

time_step = 0.2

AXES = ("row", "col")
VMEM = pltpu.VMEM


def split_kernel(slots, h_hbm, hi_ref, lo_ref, buf, sem):
    times, cols, depth, width = h_hbm.shape

    def copy(s):
        return pltpu.make_async_copy(h_hbm.at[s], buf.at[s % slots], sem.at[s % slots])

    for s in range(slots - 1):
        copy(s).start()

    def body(s, carry):
        @pl.when(s + slots - 1 < times)
        def _():
            copy(s + slots - 1).start()

        copy(s).wait()
        rows = pl.ds(pl.multiple_of(s * depth, depth), depth)
        for t in range(cols):
            tile = buf[s % slots, t]
            high = tile.astype(jnp.bfloat16)
            at = slice(t * width, (t + 1) * width)
            hi_ref[rows, at] = high
            lo_ref[rows, at] = (tile - high.astype(jnp.float32)).astype(jnp.bfloat16)
        return carry

    lax.fori_loop(0, times, body, 0)


def split_history(history):
    times, cols, depth, width = history.shape
    slots = 4
    shape = (times * depth, cols * width)
    return pl.pallas_call(
        functools.partial(split_kernel, slots),
        in_specs=[pl.BlockSpec(memory_space=pl.ANY)],
        out_specs=[pl.BlockSpec(memory_space=VMEM)] * 2,
        out_shape=[pltpu.VMEM(shape, jnp.bfloat16)] * 2,
        scratch_shapes=[
            pltpu.VMEM((slots, cols, depth, width), jnp.float32),
            pltpu.SemaphoreType.DMA((slots,)),
        ],
        compiler_params=pltpu.CompilerParams(vmem_limit_bytes=26 << 20),
        cost_estimate=pl.CostEstimate(
            flops=0, bytes_accessed=history.size * 8, transcendentals=0
        ),
        name="split_history",
    )(history)


def contract_kernel(panels, where, *refs):
    blocks = refs[:panels]
    hi_ref, lo_ref, out_ref, sig = refs[panels:]
    halves, cols, rows, depth = blocks[0].shape
    width = depth
    total = panels * rows
    for b in range(panels):
        for half in range(halves):
            at_half = where[panels + b] ^ half
            for t in range(cols):
                x = blocks[b][at_half, t]
                x = x * x * x
                high = x.astype(jnp.bfloat16)
                s = half * cols + t
                at = slice(s * depth, (s + 1) * depth)
                sig[b * rows : (b + 1) * rows, at] = high
                sig[total + b * rows : total + (b + 1) * rows, at] = (
                    x - high.astype(jnp.float32)
                ).astype(jnp.bfloat16)
    group = 4 if cols % 4 == 0 else 1
    for t0 in range(0, cols, group):
        at = slice(t0 * width, (t0 + group) * width)
        both = jnp.dot(sig[...], hi_ref[:, at], preferred_element_type=jnp.float32)
        rest = jnp.dot(
            sig[0:total, :], lo_ref[:, at], preferred_element_type=jnp.float32
        )
        value = both[0:total] + both[total:] + rest
        for b in range(panels):
            for t in range(group):
                out_ref[where[b], t0 + t] = value[
                    b * rows : (b + 1) * rows, t * width : (t + 1) * width
                ]


def contract(where, blocks, hi, lo):
    panels = len(blocks)
    halves, cols, rows, depth = blocks[0].shape
    inner, outer = hi.shape
    total = panels * rows
    return pl.pallas_call(
        functools.partial(contract_kernel, panels),
        in_specs=[pl.BlockSpec(memory_space=pltpu.SMEM)]
        + [pl.BlockSpec(memory_space=VMEM)] * (panels + 2),
        out_specs=pl.BlockSpec(memory_space=VMEM),
        out_shape=jax.ShapeDtypeStruct(
            (panels, outer // depth, rows, depth), jnp.float32
        ),
        scratch_shapes=[pltpu.VMEM((2 * total, inner), jnp.bfloat16)],
        compiler_params=pltpu.CompilerParams(vmem_limit_bytes=12 << 20),
        cost_estimate=pl.CostEstimate(
            flops=6 * total * inner * outer, bytes_accessed=4 << 20, transcendentals=0
        ),
        name="contract",
    )(where, *blocks, hi, lo)


def pairs(nrow, ncol, target):
    listed = []
    for r in range(nrow):
        for c in range(ncol):
            to_r, to_c = target(r, c // CORES, c % CORES)
            listed.append((r * ncol + c, to_r * ncol + to_c))
    return listed


def per_device(nrow, ncol, new_row, history, hamiltonian):
    def move(value, target):
        return lax.ppermute(value, AXES, pairs(nrow, ncol, target))

    def partner(value):
        return move(value, lambda r, m, k: (r, m * CORES + 1 - k))

    r = lax.axis_index("row")
    m, k = lax.axis_index("col") // CORES, lax.axis_index("col") % CORES
    turns = [(d, nrow - 1 - d) for d in range(nrow // CORES)]
    sends = [
        lambda r, m, k, turn=turn: (m, (r ^ turn[k]) * CORES + k) for turn in turns
    ]
    own = [jnp.where(k == 0, turn[0], turn[1]) for turn in turns]
    theirs = [jnp.where(k == 0, turn[1], turn[0]) for turn in turns]
    where = jnp.stack(
        [m ^ d ^ r for d in own + theirs]
        + [k for _ in own]
        + [1 - k for _ in theirs]
    ).astype(jnp.int32)

    hi, lo = split_history(history)
    current = jnp.transpose(new_row, (1, 0, 2))
    results = []
    for step_index in range(STEPS):
        both = jnp.stack([current, partner(current)])
        mine = [move(both, send) for send in sends]
        other = [partner(block) for block in mine]
        parts = contract(where, mine + other, hi, lo)
        kinetic = jnp.einsum(
            "til,lj->tij",
            current,
            hamiltonian,
            precision=lax.Precision.HIGHEST,
            preferred_element_type=jnp.float32,
        )
        collision = parts[0]
        for x in range(1, nrow):
            collision = collision + move(
                parts[x], lambda r, m, k, x=x: (r ^ x, m * CORES + k)
            )
        current = current - time_step * (kinetic + collision)
        results.append(jnp.transpose(current, (1, 0, 2)))
    return jnp.stack(results)


def solution(mesh):
    placed = (P("row", "col", None), P("row", "col", None, None), P())
    return jax.shard_map(
        functools.partial(per_device, mesh.shape["row"], mesh.shape["col"]),
        mesh=mesh,
        in_specs=placed,
        out_specs=P(None, "row", "col", None),
        check_vma=False,
    )
```

```python
import functools

import jax
import jax.numpy as jnp
from jax import lax
from jax.experimental import pallas as pl
from jax.experimental.pallas import tpu as pltpu
from jax.sharding import PartitionSpec as P


STEPS = 3
CORES = 2
CHUNKS = 2

time_step = 0.2

AXES = ("row", "col")
VMEM = pltpu.VMEM


def split_kernel(slots, h_hbm, hi_ref, lo_ref, buf, sem):
    times, cols, depth, width = h_hbm.shape
    piece = cols // CHUNKS

    def copy(s):
        return pltpu.make_async_copy(h_hbm.at[s], buf.at[s % slots], sem.at[s % slots])

    for s in range(slots - 1):
        copy(s).start()

    def body(s, carry):
        @pl.when(s + slots - 1 < times)
        def _():
            copy(s + slots - 1).start()

        copy(s).wait()
        half, t = s // cols, s % cols
        order = ((t // piece) * CORES + half) * piece + t % piece
        rows = pl.ds(pl.multiple_of(order * depth, depth), depth)
        for t in range(cols):
            tile = buf[s % slots, t]
            high = tile.astype(jnp.bfloat16)
            at = slice(t * width, (t + 1) * width)
            hi_ref[rows, at] = high
            lo_ref[rows, at] = (tile - high.astype(jnp.float32)).astype(jnp.bfloat16)
        return carry

    lax.fori_loop(0, times, body, 0)


def split_history(history):
    times, cols, depth, width = history.shape
    slots = 6
    shape = (times * depth, cols * width)
    history = pltpu.with_memory_space_constraint(history, pltpu.HBM)
    return pl.pallas_call(
        functools.partial(split_kernel, slots),
        in_specs=[pl.BlockSpec(memory_space=pltpu.HBM)],
        out_specs=[pl.BlockSpec(memory_space=VMEM)] * 2,
        out_shape=[pltpu.VMEM(shape, jnp.bfloat16)] * 2,
        scratch_shapes=[
            pltpu.VMEM((slots, cols, depth, width), jnp.float32),
            pltpu.SemaphoreType.DMA((slots,)),
        ],
        compiler_params=pltpu.CompilerParams(vmem_limit_bytes=6 << 20),
        cost_estimate=pl.CostEstimate(
            flops=0, bytes_accessed=history.size * 8, transcendentals=0
        ),
        name="split_history",
    )(history)


def position():
    r = lax.axis_index("row")
    c = lax.axis_index("col")
    return r, c // CORES, c % CORES


def origins(turns, k):
    own = [jnp.where(k == 0, turn[0], turn[1]) for turn in turns]
    theirs = [jnp.where(k == 0, turn[1], turn[0]) for turn in turns]
    return [(d, k) for d in own] + [(d, 1 - k) for d in theirs]


def fill(turns, blocks, sig):
    _, _, k = position()
    halves, cols, rows, depth = blocks[0].shape
    total = len(blocks) * rows
    for b, (_, first) in enumerate(origins(turns, k)):
        for half in range(halves):
            for t in range(cols):
                x = blocks[b][first ^ half, t]
                x = x * x * x
                high = x.astype(jnp.bfloat16)
                s = half * cols + t
                at = slice(s * depth, (s + 1) * depth)
                sig[b * rows : (b + 1) * rows, at] = high
                sig[total + b * rows : total + (b + 1) * rows, at] = (
                    x - high.astype(jnp.float32)
                ).astype(jnp.bfloat16)


def product(sig, hi, lo, inner, at):
    total = sig.shape[0] // 2
    both = jnp.dot(sig[...], hi[inner, at], preferred_element_type=jnp.float32)
    rest = jnp.dot(
        sig[0:total, :], lo[inner, at], preferred_element_type=jnp.float32
    )
    return both[0:total] + both[total:] + rest


def spread(turns, value, out, t0, group):
    r, m, k = position()
    rows, width = out.shape[2:]
    for b, (d, _) in enumerate(origins(turns, k)):
        for t in range(group):
            out[m ^ d ^ r, t0 + t] = value[
                b * rows : (b + 1) * rows, t * width : (t + 1) * width
            ]


def first_kernel(turns, panels, *refs):
    blocks = refs[:panels]
    hi, lo, acc, _, _, sig = refs[panels:]
    fill(turns, blocks, sig)
    inner = slice(0, sig.shape[1])
    step = 256
    for n in range(0, acc.shape[1], step):
        at = slice(n, n + step)
        acc[:, at] = product(sig, hi, lo, inner, at)


def second_kernel(turns, panels, *refs):
    blocks = refs[:panels]
    acc, hi, lo, out, sig, _, _ = refs[panels:]
    fill(turns, blocks, sig)
    finish(turns, 0, sig, acc, hi, lo, out)


def third_kernel(turns, sig, acc, hi, lo, out, hi_out, lo_out):
    finish(turns, 1, sig, acc, hi, lo, out)


def finish(turns, chunk, sig, acc, hi, lo, out):
    depth = sig.shape[1]
    inner = slice(depth, 2 * depth)
    cols, _, width = out.shape[1:]
    group = 2
    for t0 in range(0, cols, group):
        n = (chunk * cols + t0) * width
        at = slice(n, n + group * width)
        value = acc[:, at] + product(sig, hi, lo, inner, at)
        spread(turns, value, out, t0, group)


def call(kernel, inputs, hi, lo, outs, scratch, flops):
    count = len(inputs)
    return pl.pallas_call(
        kernel,
        in_specs=[pl.BlockSpec(memory_space=VMEM)] * (count + 2),
        out_specs=[pl.BlockSpec(memory_space=VMEM)] * (len(outs) + 2),
        out_shape=outs
        + [pltpu.VMEM(hi.shape, hi.dtype), pltpu.VMEM(lo.shape, lo.dtype)],
        input_output_aliases={count: len(outs), count + 1: len(outs) + 1},
        scratch_shapes=scratch,
        compiler_params=pltpu.CompilerParams(vmem_limit_bytes=6 << 20),
        cost_estimate=pl.CostEstimate(
            flops=flops, bytes_accessed=4 << 20, transcendentals=0
        ),
    )(*inputs, hi, lo)


def small_call(kernel, like, inputs):
    return pl.pallas_call(
        kernel,
        in_specs=[pl.BlockSpec(memory_space=VMEM)] * len(inputs),
        out_specs=pl.BlockSpec(memory_space=VMEM),
        out_shape=jax.ShapeDtypeStruct(like.shape, like.dtype),
        compiler_params=pltpu.CompilerParams(vmem_limit_bytes=4 << 20),
        cost_estimate=pl.CostEstimate(
            flops=0, bytes_accessed=1 << 20, transcendentals=0
        ),
    )(*inputs)


def base_kernel(value, hamiltonian, out):
    x = value[...]
    kinetic = jnp.dot(
        x.reshape(-1, x.shape[-1]),
        hamiltonian[...],
        precision=lax.Precision.HIGHEST,
        preferred_element_type=jnp.float32,
    )
    out[...] = x - time_step * kinetic.reshape(x.shape)


def own_kernel(base, part, out):
    out[...] = base[...] - time_step * part[...]


def pairs(nrow, ncol, target):
    listed = []
    for r in range(nrow):
        for c in range(ncol):
            to_r, to_c = target(r, c // CORES, c % CORES)
            listed.append((r * ncol + c, to_r * ncol + to_c))
    return listed


def per_device(nrow, ncol, new_row, history, hamiltonian):
    def move(value, target):
        return lax.ppermute(value, AXES, pairs(nrow, ncol, target))

    def partner(value):
        return move(value, lambda r, m, k: (r, m * CORES + 1 - k))

    turns = []
    for d in range(nrow // 4):
        turns += [(d, d ^ nrow // 2), (d ^ nrow - 1, d ^ nrow // 2 ^ nrow - 1)]
    sends = [
        lambda r, m, k, turn=turn: (m, (r ^ turn[k]) * CORES + k) for turn in turns
    ]

    def gather(value, other):
        both = jnp.stack([value, other])
        mine = [move(both, send) for send in sends]
        return mine + [partner(block) for block in mine]

    def reduce(parts):
        return [parts[0]] + [
            move(parts[x], lambda r, m, k, x=x: (r ^ x, m * CORES + k))
            for x in range(1, nrow)
        ]

    hi, lo = split_history(history)
    start = jnp.transpose(new_row, (1, 0, 2))
    cols, rows, width = start.shape
    piece = cols // CHUNKS
    swapped = partner(start)
    state = [start[a * piece : (a + 1) * piece] for a in range(CHUNKS)]
    other = [swapped[a * piece : (a + 1) * piece] for a in range(CHUNKS)]
    total = nrow * rows
    depth = hi.shape[0] // CHUNKS
    part = jax.ShapeDtypeStruct((nrow, piece, rows, width), jnp.float32)
    acc_type = jax.ShapeDtypeStruct((total, hi.shape[1]), jnp.float32)
    sig_type = jax.ShapeDtypeStruct((2 * total, depth), jnp.bfloat16)
    flops = 3 * total * depth * hi.shape[1]
    rows_out = jnp.zeros((STEPS, cols, rows, width), jnp.float32)
    for n in range(STEPS):
        if n > 0:
            other = [partner(state[a]) for a in range(CHUNKS)]
        blocks = [gather(state[a], other[a]) for a in range(CHUNKS)]
        base = []
        for value in state:
            base.append(small_call(base_kernel, value, [value, hamiltonian]))
        acc, hi, lo = call(
            functools.partial(first_kernel, turns, nrow),
            blocks[0], hi, lo, [acc_type],
            [pltpu.VMEM(sig_type.shape, sig_type.dtype)], 2 * flops,
        )
        parts0, sig, hi, lo = call(
            functools.partial(second_kernel, turns, nrow),
            blocks[1] + [acc], hi, lo, [part, sig_type], [], flops,
        )
        parts1, hi, lo = call(
            functools.partial(third_kernel, turns),
            [sig, acc], hi, lo, [part], [], flops,
        )
        base[0] = small_call(own_kernel, state[0], [base[0], parts0[0]])
        for a, parts in enumerate((parts0, parts1)):
            arrived = reduce(parts)
            total = sum(arrived[2:], arrived[1])
            if a:
                total = total + arrived[0]
            state[a] = base[a] - time_step * total
            rows_out = lax.dynamic_update_slice(
                rows_out, state[a][None], (n, a * piece, 0, 0)
            )
    return jnp.transpose(rows_out, (0, 2, 1, 3))


def solution(mesh):
    placed = (P("row", "col", None), P("row", "col", None, None), P())
    return jax.shard_map(
        functools.partial(per_device, mesh.shape["row"], mesh.shape["col"]),
        mesh=mesh,
        in_specs=placed,
        out_specs=P(None, "row", "col", None),
        check_vma=False,
    )
```

```python
import functools

import jax
import jax.numpy as jnp
from jax import lax
from jax.experimental import pallas as pl
from jax.experimental.pallas import tpu as pltpu
from jax.sharding import PartitionSpec as P


STEPS = 3
CORES = 2
CHUNKS = 2

time_step = 0.2

AXES = ("row", "col")
VMEM = pltpu.VMEM


def split_kernel(slots, h_hbm, hi_ref, lo_ref, buf, sem):
    times, cols, depth, width = h_hbm.shape

    def copy(s):
        return pltpu.make_async_copy(h_hbm.at[s], buf.at[s % slots], sem.at[s % slots])

    for s in range(slots - 1):
        copy(s).start()

    def body(s, carry):
        @pl.when(s + slots - 1 < times)
        def _():
            copy(s + slots - 1).start()

        copy(s).wait()
        rows = pl.ds(pl.multiple_of(s * depth, depth), depth)
        for t in range(cols):
            tile = buf[s % slots, t]
            high = tile.astype(jnp.bfloat16)
            at = slice(t * width, (t + 1) * width)
            hi_ref[rows, at] = high
            lo_ref[rows, at] = (tile - high.astype(jnp.float32)).astype(jnp.bfloat16)
        return carry

    lax.fori_loop(0, times, body, 0)


def split_history(history):
    times, cols, depth, width = history.shape
    slots = 6
    shape = (times * depth, cols * width)
    history = pltpu.with_memory_space_constraint(history, pltpu.HBM)
    return pl.pallas_call(
        functools.partial(split_kernel, slots),
        in_specs=[pl.BlockSpec(memory_space=pltpu.HBM)],
        out_specs=[pl.BlockSpec(memory_space=VMEM)] * 2,
        out_shape=[pltpu.VMEM(shape, jnp.bfloat16)] * 2,
        scratch_shapes=[
            pltpu.VMEM((slots, cols, depth, width), jnp.float32),
            pltpu.SemaphoreType.DMA((slots,)),
        ],
        compiler_params=pltpu.CompilerParams(vmem_limit_bytes=6 << 20),
        cost_estimate=pl.CostEstimate(
            flops=0, bytes_accessed=history.size * 8, transcendentals=0
        ),
        name="split_history",
    )(history)


def position():
    r = lax.axis_index("row")
    c = lax.axis_index("col")
    return r, c // CORES, c % CORES


def origins(turns, k):
    own = [jnp.where(k == 0, turn[0], turn[1]) for turn in turns]
    theirs = [jnp.where(k == 0, turn[1], turn[0]) for turn in turns]
    return [(d, k) for d in own] + [(d, 1 - k) for d in theirs]


def fill(turns, blocks, sig):
    _, _, k = position()
    halves, cols, rows, depth = blocks[0].shape
    total = len(blocks) * rows
    for b, (_, first) in enumerate(origins(turns, k)):
        for half in range(halves):
            for t in range(cols):
                x = blocks[b][first ^ half, t]
                x = x * x * x
                high = x.astype(jnp.bfloat16)
                s = half * cols + t
                at = slice(s * depth, (s + 1) * depth)
                sig[b * rows : (b + 1) * rows, at] = high
                sig[total + b * rows : total + (b + 1) * rows, at] = (
                    x - high.astype(jnp.float32)
                ).astype(jnp.bfloat16)


def spread(turns, value, out, t0, group):
    r, m, k = position()
    rows, width = out.shape[2:]
    for b, (d, _) in enumerate(origins(turns, k)):
        for t in range(group):
            out[m ^ d ^ r, t0 + t] = value[
                b * rows : (b + 1) * rows, t * width : (t + 1) * width
            ]


def contract_kernel(turns, panels, *refs):
    blocks = refs[:panels]
    hi, lo, out, _, _, sig = refs[panels:]
    fill(turns, blocks, sig)
    total = sig.shape[0] // 2
    cols, _, width = out.shape[1:]
    group = 4 if cols % 4 == 0 else 1
    for t0 in range(0, cols, group):
        at = slice(t0 * width, (t0 + group) * width)
        both = jnp.dot(sig[...], hi[:, at], preferred_element_type=jnp.float32)
        rest = jnp.dot(
            sig[0:total, :], lo[:, at], preferred_element_type=jnp.float32
        )
        spread(turns, both[0:total] + both[total:] + rest, out, t0, group)


def call(kernel, inputs, hi, lo, outs, scratch, flops):
    count = len(inputs)
    return pl.pallas_call(
        kernel,
        in_specs=[pl.BlockSpec(memory_space=VMEM)] * (count + 2),
        out_specs=[pl.BlockSpec(memory_space=VMEM)] * (len(outs) + 2),
        out_shape=outs
        + [pltpu.VMEM(hi.shape, hi.dtype), pltpu.VMEM(lo.shape, lo.dtype)],
        input_output_aliases={count: len(outs), count + 1: len(outs) + 1},
        scratch_shapes=scratch,
        compiler_params=pltpu.CompilerParams(vmem_limit_bytes=6 << 20),
        cost_estimate=pl.CostEstimate(
            flops=flops, bytes_accessed=4 << 20, transcendentals=0
        ),
    )(*inputs, hi, lo)


def small_call(kernel, like, inputs):
    return pl.pallas_call(
        kernel,
        in_specs=[pl.BlockSpec(memory_space=VMEM)] * len(inputs),
        out_specs=pl.BlockSpec(memory_space=VMEM),
        out_shape=jax.ShapeDtypeStruct(like.shape, like.dtype),
        compiler_params=pltpu.CompilerParams(vmem_limit_bytes=4 << 20),
        cost_estimate=pl.CostEstimate(
            flops=0, bytes_accessed=1 << 20, transcendentals=0
        ),
    )(*inputs)


def base_kernel(value, hamiltonian, out):
    x = value[...]
    kinetic = jnp.dot(
        x.reshape(-1, x.shape[-1]),
        hamiltonian[...],
        precision=lax.Precision.HIGHEST,
        preferred_element_type=jnp.float32,
    )
    out[...] = x - time_step * kinetic.reshape(x.shape)


def own_kernel(base, part, out):
    out[...] = base[...] - time_step * part[...]


def pairs(nrow, ncol, target):
    listed = []
    for r in range(nrow):
        for c in range(ncol):
            to_r, to_c = target(r, c // CORES, c % CORES)
            listed.append((r * ncol + c, to_r * ncol + to_c))
    return listed


def per_device(nrow, ncol, new_row, history, hamiltonian):
    def move(value, target):
        return lax.ppermute(value, AXES, pairs(nrow, ncol, target))

    def partner(value):
        return move(value, lambda r, m, k: (r, m * CORES + 1 - k))

    turns = [(nrow - 1 - d, d) for d in range(nrow // CORES)]
    sends = [
        lambda r, m, k, turn=turn: (m, (r ^ turn[k]) * CORES + k) for turn in turns
    ]

    def gather(value, other):
        both = jnp.stack([value, other])
        mine = [move(both, send) for send in sends]
        return mine + [partner(block) for block in mine]

    def reduce(parts):
        return [
            move(parts[x], lambda r, m, k, x=x: (r ^ x, m * CORES + k))
            for x in range(1, nrow)
        ]

    hi, lo = split_history(history)
    start = jnp.transpose(new_row, (1, 0, 2))
    cols, rows, width = start.shape
    piece = rows // CHUNKS
    swapped = partner(start)
    state = [start[:, a * piece : (a + 1) * piece] for a in range(CHUNKS)]
    other = [swapped[:, a * piece : (a + 1) * piece] for a in range(CHUNKS)]
    total = nrow * piece
    inner, outer = hi.shape
    parts_type = jax.ShapeDtypeStruct((nrow, cols, piece, width), jnp.float32)
    rows_out = jnp.zeros((STEPS, cols, rows, width), jnp.float32)
    for n in range(STEPS):
        for a in range(CHUNKS):
            if n > 0:
                other[a] = partner(state[a])
            blocks = gather(state[a], other[a])
            base = small_call(base_kernel, state[a], [state[a], hamiltonian])
            parts, hi, lo = call(
                functools.partial(contract_kernel, turns, nrow),
                blocks, hi, lo, [parts_type],
                [pltpu.VMEM((2 * total, inner), jnp.bfloat16)],
                6 * total * inner * outer,
            )
            base = small_call(own_kernel, state[a], [base, parts[0]])
            arrived = reduce(parts)
            state[a] = base - time_step * sum(arrived[1:], arrived[0])
            rows_out = lax.dynamic_update_slice(
                rows_out, state[a][None], (n, 0, a * piece, 0)
            )
    return jnp.transpose(rows_out, (0, 2, 1, 3))


def solution(mesh):
    placed = (P("row", "col", None), P("row", "col", None, None), P())
    return jax.shard_map(
        functools.partial(per_device, mesh.shape["row"], mesh.shape["col"]),
        mesh=mesh,
        in_specs=placed,
        out_specs=P(None, "row", "col", None),
        check_vma=False,
    )
```

```python
import functools

import jax
import jax.numpy as jnp
from jax import lax
from jax.experimental import pallas as pl
from jax.experimental.pallas import tpu as pltpu
from jax.sharding import PartitionSpec as P


STEPS = 3
CORES = 2
CHUNKS = 2

time_step = 0.2

LARGEST = float(jnp.finfo(jnp.bfloat16).max)

AXES = ("row", "col")
VMEM = pltpu.VMEM


def split_kernel(slots, h_hbm, hi_ref, lo_ref, buf, sem):
    times, cols, depth, width = h_hbm.shape

    def copy(s):
        return pltpu.make_async_copy(h_hbm.at[s], buf.at[s % slots], sem.at[s % slots])

    for s in range(slots - 1):
        copy(s).start()

    def body(s, carry):
        @pl.when(s + slots - 1 < times)
        def _():
            copy(s + slots - 1).start()

        copy(s).wait()
        rows = pl.ds(pl.multiple_of(s * depth, depth), depth)
        for t in range(cols):
            tile = buf[s % slots, t]
            high = tile.astype(jnp.bfloat16)
            at = slice(t * width, (t + 1) * width)
            hi_ref[rows, at] = high
            lo_ref[rows, at] = (tile - high.astype(jnp.float32)).astype(jnp.bfloat16)
        return carry

    lax.fori_loop(0, times, body, 0)


def split_history(history):
    times, cols, depth, width = history.shape
    slots = 6
    shape = (times * depth, cols * width)
    history = pltpu.with_memory_space_constraint(history, pltpu.HBM)
    return pl.pallas_call(
        functools.partial(split_kernel, slots),
        in_specs=[pl.BlockSpec(memory_space=pltpu.HBM)],
        out_specs=[pl.BlockSpec(memory_space=VMEM)] * 2,
        out_shape=[pltpu.VMEM(shape, jnp.bfloat16)] * 2,
        scratch_shapes=[
            pltpu.VMEM((slots, cols, depth, width), jnp.float32),
            pltpu.SemaphoreType.DMA((slots,)),
        ],
        compiler_params=pltpu.CompilerParams(vmem_limit_bytes=6 << 20),
        cost_estimate=pl.CostEstimate(
            flops=0, bytes_accessed=history.size * 8, transcendentals=0
        ),
        name="split_history",
    )(history)


def position():
    r = lax.axis_index("row")
    c = lax.axis_index("col")
    return r, c // CORES, c % CORES


def origins(turns, k):
    own = [jnp.where(k == 0, turn[0], turn[1]) for turn in turns]
    theirs = [jnp.where(k == 0, turn[1], turn[0]) for turn in turns]
    return [(d, k) for d in own] + [(d, 1 - k) for d in theirs]


def fill(turns, blocks, sig):
    _, _, k = position()
    halves, cols, rows, depth = blocks[0].shape
    total = len(blocks) * rows
    for b, (_, first) in enumerate(origins(turns, k)):
        for half in range(halves):
            for t in range(cols):
                x = blocks[b][first ^ half, t]
                x = x * x * x
                high = jnp.clip(x, -LARGEST, LARGEST).astype(jnp.bfloat16)
                s = half * cols + t
                at = slice(s * depth, (s + 1) * depth)
                sig[b * rows : (b + 1) * rows, at] = high
                sig[total + b * rows : total + (b + 1) * rows, at] = (
                    x - high.astype(jnp.float32)
                ).astype(jnp.bfloat16)


def spread(turns, value, out, t0, group):
    r, m, k = position()
    rows, width = out.shape[2:]
    for b, (d, _) in enumerate(origins(turns, k)):
        for t in range(group):
            out[m ^ d ^ r, t0 + t] = value[
                b * rows : (b + 1) * rows, t * width : (t + 1) * width
            ]


def contract_kernel(turns, panels, *refs):
    blocks = refs[:panels]
    hi, lo, out, _, _, sig = refs[panels:]
    fill(turns, blocks, sig)
    total = sig.shape[0] // 2
    cols, _, width = out.shape[1:]
    group = cols
    for t0 in range(0, cols, group):
        at = slice(t0 * width, (t0 + group) * width)
        both = jnp.dot(sig[...], hi[:, at], preferred_element_type=jnp.float32)
        rest = jnp.dot(
            sig[0:total, :], lo[:, at], preferred_element_type=jnp.float32
        )
        spread(turns, both[0:total] + both[total:] + rest, out, t0, group)


def call(kernel, inputs, hi, lo, outs, scratch, flops):
    count = len(inputs)
    return pl.pallas_call(
        kernel,
        in_specs=[pl.BlockSpec(memory_space=VMEM)] * (count + 2),
        out_specs=[pl.BlockSpec(memory_space=VMEM)] * (len(outs) + 2),
        out_shape=outs
        + [pltpu.VMEM(hi.shape, hi.dtype), pltpu.VMEM(lo.shape, lo.dtype)],
        input_output_aliases={count: len(outs), count + 1: len(outs) + 1},
        scratch_shapes=scratch,
        compiler_params=pltpu.CompilerParams(vmem_limit_bytes=6 << 20),
        cost_estimate=pl.CostEstimate(
            flops=flops, bytes_accessed=4 << 20, transcendentals=0
        ),
    )(*inputs, hi, lo)


def small_call(kernel, like, inputs):
    return pl.pallas_call(
        kernel,
        in_specs=[pl.BlockSpec(memory_space=VMEM)] * len(inputs),
        out_specs=pl.BlockSpec(memory_space=VMEM),
        out_shape=jax.ShapeDtypeStruct(like.shape, like.dtype),
        compiler_params=pltpu.CompilerParams(vmem_limit_bytes=4 << 20),
        cost_estimate=pl.CostEstimate(
            flops=0, bytes_accessed=1 << 20, transcendentals=0
        ),
    )(*inputs)


def base_kernel(value, hamiltonian, out):
    x = value[...]
    kinetic = jnp.dot(
        x.reshape(-1, x.shape[-1]),
        hamiltonian[...],
        precision=lax.Precision.HIGHEST,
        preferred_element_type=jnp.float32,
    )
    out[...] = x - time_step * kinetic.reshape(x.shape)


def own_kernel(base, part, out):
    out[...] = base[...] - time_step * part[...]


def pairs(nrow, ncol, target):
    listed = []
    for r in range(nrow):
        for c in range(ncol):
            to_r, to_c = target(r, c // CORES, c % CORES)
            listed.append((r * ncol + c, to_r * ncol + to_c))
    return listed


def per_device(nrow, ncol, new_row, history, hamiltonian):
    def move(value, target):
        return lax.ppermute(value, AXES, pairs(nrow, ncol, target))

    def partner(value):
        return move(value, lambda r, m, k: (r, m * CORES + 1 - k))

    turns = [(nrow - 1 - d, d) for d in range(nrow // CORES)]
    sends = [
        lambda r, m, k, turn=turn: (m, (r ^ turn[k]) * CORES + k) for turn in turns
    ]

    def gather(value, other):
        both = jnp.stack([value, other])
        mine = [move(both, send) for send in sends]
        return mine + [partner(block) for block in mine]

    def reduce(parts):
        return [
            move(parts[x], lambda r, m, k, x=x: (r ^ x, m * CORES + k))
            for x in range(1, nrow)
        ]

    hi, lo = split_history(history)
    start = jnp.transpose(new_row, (1, 0, 2))
    cols, rows, width = start.shape
    piece = rows // CHUNKS
    swapped = partner(start)
    state = [start[:, a * piece : (a + 1) * piece] for a in range(CHUNKS)]
    other = [swapped[:, a * piece : (a + 1) * piece] for a in range(CHUNKS)]
    total = nrow * piece
    inner, outer = hi.shape
    parts_type = jax.ShapeDtypeStruct((nrow, cols, piece, width), jnp.float32)
    rows_out = jnp.zeros((STEPS, cols, rows, width), jnp.float32)
    for n in range(STEPS):
        for a in range(CHUNKS):
            if n > 0:
                other[a] = partner(state[a])
            blocks = gather(state[a], other[a])
            base = small_call(base_kernel, state[a], [state[a], hamiltonian])
            parts, hi, lo = call(
                functools.partial(contract_kernel, turns, nrow),
                blocks, hi, lo, [parts_type],
                [pltpu.VMEM((2 * total, inner), jnp.bfloat16)],
                6 * total * inner * outer,
            )
            base = small_call(own_kernel, state[a], [base, parts[0]])
            arrived = reduce(parts)
            state[a] = base - time_step * sum(arrived[1:], arrived[0])
            rows_out = lax.dynamic_update_slice(
                rows_out, state[a][None], (n, 0, a * piece, 0)
            )
    return jnp.transpose(rows_out, (0, 2, 1, 3))


def solution(mesh):
    placed = (P("row", "col", None), P("row", "col", None, None), P())
    return jax.shard_map(
        functools.partial(per_device, mesh.shape["row"], mesh.shape["col"]),
        mesh=mesh,
        in_specs=placed,
        out_specs=P(None, "row", "col", None),
        check_vma=False,
    )
```
